32 devices in a mesh: isl: 4 (over x, core), fsdp: 8 (over z, y).
Axes of the slice: x: 2, y: 2, z: 4, core: 2. Of those that a mesh axis runs over, the one named last changes fastest.
Arguments:
- weights: float32 [3, 7168, 4096], P(None, 'fsdp', 'isl'), may hold values from -6 to 6
- momentum: float32 [3, 7168, 4096], P(None, 'fsdp', 'isl'), may hold values from -0.12 to 0.12
- first_moment: bfloat16 [4, 3, 7168, 4096], P('isl', None, 'fsdp'), may hold values from -0.00029945374 to 0.00029945374
- second_moment: bfloat16 [4, 3, 7168, 4096], P('isl', None, 'fsdp'), may hold values from 9.95351e-09 to 9.953976e-06
- inputs: bfloat16 [2, 256, 4096], P(None, ('isl', 'fsdp')), may hold values from -6 to 6
- targets: bfloat16 [2, 256, 4096], P(None, ('isl', 'fsdp')), may hold values from -6 to 6
- overflow_step: int32 [4, 8], P('isl', 'fsdp'), may hold values from 0 to 15
Outputs:
- new_weights: float32 [3, 7168, 4096], P(None, 'fsdp', 'isl')
- new_momentum: float32 [3, 7168, 4096], P(None, 'fsdp', 'isl')
The draws below stay inside these ranges and needn't reach their ends.
Inputs may be any that keep to these rules, and one draw needn't show every extreme that they name: `overflow_step`: A device reports an overflow at inner step k when its value equals k; values of 2 or more report none.
All inputs are finite; a program needn't handle non-finite values.
Results may differ from the reference program's by a relative error of at most 0.004.
Values may be sent and summed in bfloat16 or wider, within the bound.
A program may use at most 320 MiB of HBM per device.

```python
import math
import jax
import jax.numpy as jnp
from jax import lax

D = 4096
FF = 7168
TOK_DEV = 8
INNER = 2
TOKENS = 256
N_ISL = 4
N_FSDP = 8


def set_ends(drawn, key, least, high):
    longest = drawn.shape.index(max(drawn.shape))
    spots = []
    for shift in (0, 1):
        where = [jax.random.randint(jax.random.fold_in(key, axis), (), 0, length) for axis, length in enumerate(drawn.shape)]
        where[longest] = (where[longest] + shift) % drawn.shape[longest]
        spots.append(tuple(where))
    return drawn.at[spots[0]].set(least).at[spots[1]].set(high)


def block_scale(rng, extent, pieces, low, largest):
    factor_of, own = 1.0, jax.random.fold_in(rng, 6)
    for position, blocks in pieces:
        heights = jnp.exp(jax.random.uniform(jax.random.fold_in(own, position), (blocks,), jnp.float32, low / len(pieces), largest / len(pieces)))
        factor_of = factor_of * jnp.repeat(heights, extent[position] // blocks).reshape([-1 if axis == position else 1 for axis in range(len(extent))])
    return factor_of


def bell_draw(stream_key, dims, deviation, reach, pieces=(), held_as=jnp.bfloat16):
    drawn = deviation * jax.random.normal(stream_key, dims, jnp.float32)
    if pieces:
        drawn = drawn * block_scale(stream_key, dims, pieces, -0.22, 0.18)
    return jnp.clip(drawn, -reach, reach).astype(held_as)


def setup_inputs(seed: int = 0) -> dict:
    key_of = jax.random.split(jax.random.key(seed), 8)
    weights = bell_draw(key_of[0], (3, FF, D), 1.0, 6.0, ((1, 8), (2, 4)), jnp.float32)
    momentum = bell_draw(key_of[1], (3, FF, D), 0.02, 0.12, ((1, 8), (2, 4)), jnp.float32)
    first_moment = bell_draw(key_of[2], (N_ISL, 3, FF, D), 0.00005, 0.00029945374, ((0, 4), (2, 8)))
    second_moment = jnp.clip(jnp.exp(math.log(9.953975677490234e-06) - 6.907802 * jax.random.uniform(key_of[3], (N_ISL, 3, FF, D), jnp.float32) ** block_scale(key_of[3], (N_ISL, 3, FF, D), ((0, 4), (2, 8)), -0.2, 0.2)), 9.953510016202927e-09, 9.953975677490234e-06).astype(jnp.bfloat16)
    inputs = bell_draw(key_of[4], (INNER, TOKENS, D), 1.0, 6.0, ((1, 32),))
    targets = bell_draw(key_of[5], (INNER, TOKENS, D), 1.0, 6.0, ((1, 32),))
    overflow_step = set_ends(jax.random.randint(key_of[6], (N_ISL, N_FSDP), 0, 2 * N_FSDP), jax.random.fold_in(key_of[6], 1), 0, (2 * N_FSDP) - 1).astype(jnp.int32)
    return {"weights": weights, "momentum": momentum, "first_moment": first_moment, "second_moment": second_moment, "inputs": inputs, "targets": targets, "overflow_step": overflow_step}


inner_rate = 0.02
beta_first = 0.9
beta_second = 0.95
epsilon = 1e-08
decay_rate = 0.1
outer_rate = 0.7
nesterov_coef = 0.9

def silu_parts(preact):
    sigmoid_value = jax.nn.sigmoid(preact)
    return (preact * sigmoid_value, sigmoid_value * (1.0 + preact * (1.0 - sigmoid_value)))

def island_gradient(rounded, block_inputs, block_targets):
    token_count = block_inputs.shape[0]
    gate_pre = jnp.dot(block_inputs, rounded[0].T, preferred_element_type=jnp.float32) / math.sqrt(D)
    up_pre = jnp.dot(block_inputs, rounded[1].T, preferred_element_type=jnp.float32) / math.sqrt(D)
    activated, slope = silu_parts(gate_pre)
    hidden = (activated * up_pre).astype(jnp.bfloat16)
    summed = jnp.dot(hidden, rounded[2], preferred_element_type=jnp.float32)
    outputs = block_inputs.astype(jnp.float32) + summed / math.sqrt(FF)
    slopes = ((outputs - block_targets.astype(jnp.float32)) / token_count).astype(jnp.bfloat16)
    hidden_slope = jnp.dot(slopes, rounded[2].T, preferred_element_type=jnp.float32) / math.sqrt(FF)
    gate_slope = (hidden_slope * up_pre * slope).astype(jnp.bfloat16)
    up_slope = (hidden_slope * activated).astype(jnp.bfloat16)
    grad_gate = jnp.dot(gate_slope.T, block_inputs, preferred_element_type=jnp.float32) / math.sqrt(D)
    grad_up = jnp.dot(up_slope.T, block_inputs, preferred_element_type=jnp.float32) / math.sqrt(D)
    grad_down = jnp.dot(hidden.T, slopes, preferred_element_type=jnp.float32) / math.sqrt(FF)
    return jnp.stack([grad_gate, grad_up, grad_down])

def reference(weights, momentum, first_moment, second_moment, inputs, targets, overflow_step):
    island_tokens = TOK_DEV * N_FSDP
    pseudo_sum = jnp.zeros(weights.shape, jnp.float32)
    for island in range(N_ISL):
        current = weights
        moment_one = first_moment[island].astype(jnp.float32)
        moment_two = second_moment[island].astype(jnp.float32)
        for inner_step in range(INNER):
            begin = island * island_tokens
            block_inputs = inputs[inner_step, begin:begin + island_tokens]
            block_targets = targets[inner_step, begin:begin + island_tokens]
            gradient = island_gradient(current.astype(jnp.bfloat16), block_inputs, block_targets)
            overflow_count = jnp.sum((overflow_step[island] == inner_step).astype(jnp.int32))
            skipped = overflow_count > 0
            next_one = beta_first * moment_one + (1.0 - beta_first) * gradient
            next_two = beta_second * moment_two + (1.0 - beta_second) * gradient * gradient
            next_weights = current - inner_rate * (next_one / (jnp.sqrt(next_two) + epsilon) + decay_rate * current)
            current = jnp.where(skipped, current, next_weights)
            moment_one = jnp.where(skipped, moment_one, next_one)
            moment_two = jnp.where(skipped, moment_two, next_two)
        pseudo = (weights - current).astype(jnp.bfloat16)
        pseudo_sum = pseudo_sum + lax.optimization_barrier(pseudo).astype(jnp.float32)
    outer_delta = pseudo_sum / N_ISL
    new_momentum = nesterov_coef * momentum + outer_delta
    new_weights = weights - outer_rate * (outer_delta + nesterov_coef * new_momentum)
    return (new_weights, new_momentum)
```

```python
import functools
import math

import jax
import jax.numpy as jnp
from jax import lax
from jax.experimental import pallas as pl
from jax.experimental.pallas import tpu as pltpu
from jax.sharding import PartitionSpec as P

MESH = pl.DeviceIdType.MESH

inner_rate = 0.02
beta_first = 0.9
beta_second = 0.95
epsilon = 1e-08
decay_rate = 0.1
outer_rate = 0.7
nesterov_coef = 0.9


def silu_parts(preact):
    sigmoid_value = jax.nn.sigmoid(preact)
    return (preact * sigmoid_value, sigmoid_value * (1.0 + preact * (1.0 - sigmoid_value)))


def contract_last(left_side, right_side):
    return lax.dot_general(
        left_side, right_side, (((1,), (1,)), ((), ())), preferred_element_type=jnp.float32
    )


def enter(peers):
    barrier = pltpu.get_barrier_semaphore()
    for peer in peers:
        pl.semaphore_signal(barrier, inc=1, device_id=peer, device_id_type=MESH)
    pl.semaphore_wait(barrier, len(peers))


def gather_kernel(n, n_isl, x_ref, flag_ref, out_ref, count_ref, got, flags, counts, own,
                  send_sem, recv_sem, fsend_sem, frecv_sem, csend_sem, crecv_sem):
    isl = lax.axis_index("isl")
    me = lax.axis_index("fsdp")
    enter(
        [{"fsdp": lax.rem(me + d, n)} for d in range(1, n)]
        + [{"isl": lax.rem(isl + d, n_isl)} for d in range(1, n_isl)]
    )
    copies = []
    for d in range(1, n):
        to = {"fsdp": lax.rem(me + d, n)}
        small = pltpu.make_async_remote_copy(
            flag_ref, flags.at[d - 1], fsend_sem.at[d - 1], frecv_sem.at[d - 1],
            device_id=to, device_id_type=MESH)
        small.start()
        big = pltpu.make_async_remote_copy(
            x_ref, got.at[d - 1], send_sem.at[d - 1], recv_sem.at[d - 1],
            device_id=to, device_id_type=MESH)
        big.start()
        copies.append((small, big))
    total = flag_ref[...]
    for d in range(1, n):
        copies[d - 1][0].wait()
        total = total + flags[d - 1]
    own[...] = total
    sent = []
    for d in range(1, n_isl):
        copy = pltpu.make_async_remote_copy(
            own, counts.at[d - 1], csend_sem.at[d - 1], crecv_sem.at[d - 1],
            device_id={"isl": lax.rem(isl + d, n_isl)}, device_id_type=MESH)
        copy.start()
        sent.append(copy)
    count_ref[0] = total
    for k in range(x_ref.shape[0]):
        out_ref[k, me] = x_ref[k]
    for d in range(1, n):
        copies[d - 1][1].wait()
        for k in range(x_ref.shape[0]):
            out_ref[k, lax.rem(me + n - d, n)] = got[d - 1, k]
    for d in range(1, n_isl):
        sent[d - 1].wait()
        count_ref[d] = counts[d - 1]


def gather_inputs(x, flags, n, n_isl):
    steps, rows, width = x.shape
    vmem = pl.BlockSpec(memory_space=pltpu.VMEM)
    return pl.pallas_call(
        functools.partial(gather_kernel, n, n_isl),
        out_shape=(jax.ShapeDtypeStruct((steps, n, rows, width), x.dtype),
                   jax.ShapeDtypeStruct((n_isl, 8, 128), jnp.float32)),
        in_specs=[vmem, vmem],
        out_specs=(vmem, vmem),
        scratch_shapes=[
            pltpu.VMEM((n - 1, steps, rows, width), x.dtype),
            pltpu.VMEM((n - 1, 8, 128), jnp.float32),
            pltpu.VMEM((n_isl - 1, 8, 128), jnp.float32),
            pltpu.VMEM((8, 128), jnp.float32),
            pltpu.SemaphoreType.DMA((n - 1,)),
            pltpu.SemaphoreType.DMA((n - 1,)),
            pltpu.SemaphoreType.DMA((n - 1,)),
            pltpu.SemaphoreType.DMA((n - 1,)),
            pltpu.SemaphoreType.DMA((n_isl - 1,)),
            pltpu.SemaphoreType.DMA((n_isl - 1,)),
        ],
        compiler_params=pltpu.CompilerParams(
            collective_id=0, has_side_effects=True, vmem_limit_bytes=40 << 20),
        name="gather_inputs",
    )(x, flags)


def slopes_kernel(n, scale, inverse, part_ref, x_ref, y_ref, out_ref, got, own, back,
                  send_sem, recv_sem, send_two, recv_two):
    me = lax.axis_index("fsdp")
    enter([{"fsdp": lax.rem(me + d, n)} for d in range(1, n)])
    copies = []
    for d in range(1, n):
        peer = lax.rem(me + d, n)
        copy = pltpu.make_async_remote_copy(
            part_ref.at[peer], got.at[d - 1], send_sem.at[d - 1], recv_sem.at[d - 1],
            device_id={"fsdp": peer}, device_id_type=MESH)
        copy.start()
        copies.append(copy)
    total = part_ref[me].astype(jnp.float32)
    for d in range(1, n):
        copies[d - 1].wait()
        total = total + got[d - 1].astype(jnp.float32)
    outputs = x_ref[...].astype(jnp.float32) + total * scale
    own[...] = ((outputs - y_ref[...].astype(jnp.float32)) * inverse).astype(jnp.bfloat16)
    copies = []
    for d in range(1, n):
        copy = pltpu.make_async_remote_copy(
            own, back.at[d - 1], send_two.at[d - 1], recv_two.at[d - 1],
            device_id={"fsdp": lax.rem(me + d, n)}, device_id_type=MESH)
        copy.start()
        copies.append(copy)
    out_ref[me] = own[...]
    for d in range(1, n):
        copies[d - 1].wait()
        out_ref[lax.rem(me + n - d, n)] = back[d - 1]


def island_slopes(part, x, y, hidden_units):
    n, rows, width = part.shape
    vmem = pl.BlockSpec(memory_space=pltpu.VMEM)
    return pl.pallas_call(
        functools.partial(
            slopes_kernel, n, 1.0 / math.sqrt(hidden_units), 1.0 / (n * rows)),
        out_shape=jax.ShapeDtypeStruct((n, rows, width), jnp.bfloat16),
        in_specs=[vmem] * 3,
        out_specs=vmem,
        scratch_shapes=[
            pltpu.VMEM((n - 1, rows, width), part.dtype),
            pltpu.VMEM((rows, width), jnp.bfloat16),
            pltpu.VMEM((n - 1, rows, width), jnp.bfloat16),
            pltpu.SemaphoreType.DMA((n - 1,)),
            pltpu.SemaphoreType.DMA((n - 1,)),
            pltpu.SemaphoreType.DMA((n - 1,)),
            pltpu.SemaphoreType.DMA((n - 1,)),
        ],
        compiler_params=pltpu.CompilerParams(
            collective_id=1, has_side_effects=True, vmem_limit_bytes=40 << 20),
        name="island_slopes",
    )(part, x, y)


def first_kernel(width, coef_ref, m_ref, v_ref, lhs_ref, rhs_ref, out_ref):
    k = pl.program_id(0)
    grad_m, grad_v = coef_ref[k, 0], coef_ref[k, 1]
    eps, factor = coef_ref[k, 2], coef_ref[k, 3]
    lhs = lhs_ref[0]
    for start in range(0, m_ref.shape[2], width):
        cols = pl.ds(start, width)
        grad = jnp.dot(lhs, rhs_ref[0, :, cols], preferred_element_type=jnp.float32)
        first = m_ref[0, :, cols].astype(jnp.float32) + grad_m * grad
        second = v_ref[0, :, cols].astype(jnp.float32) + grad_v * (grad * grad)
        root = second * lax.rsqrt(second) + eps
        out_ref[0, :, cols] = (factor * first / root).astype(jnp.bfloat16)


def first_update(coefs, m, v, lhs, rhs):
    mats, rows, width = m.shape
    tokens = lhs.shape[2]
    tile = next(t for t in (128, 64, 32, 16, 8) if rows % t == 0)
    block = pl.BlockSpec((1, tile, width), lambda k, r: (k, r, 0))
    return pl.pallas_call(
        functools.partial(first_kernel, min(256, width)),
        grid=(mats, rows // tile),
        out_shape=jax.ShapeDtypeStruct(m.shape, jnp.bfloat16),
        in_specs=[
            pl.BlockSpec(memory_space=pltpu.SMEM),
            block,
            block,
            pl.BlockSpec((1, tile, tokens), lambda k, r: (k, r, 0)),
            pl.BlockSpec((1, tokens, width), lambda k, r: (k // 2, 0, 0)),
        ],
        out_specs=block,
        compiler_params=pltpu.CompilerParams(
            dimension_semantics=("arbitrary", "arbitrary"), vmem_limit_bytes=40 << 20),
        name="first_update",
    )(coefs, m, v, lhs, rhs)


SLOTS = 8
LAG = 4


def last_kernel(chunks, per, tile, quarter, width, coef_ref, m_ref, v_ref, p_ref, lhs0_ref,
                lhs1_ref, rhs0_ref, rhs1_ref, w_ref, mom_ref, neww_ref, newm_ref,
                keep, send_a, recv_a, near, send_b, recv_b,
                sa_sem, ra_sem, sb_sem, rb_sem, credit_a, credit_b):
    t = pl.program_id(0)
    me = lax.axis_index("isl")
    side, core = me // 2, lax.rem(me, 2)
    partner = {"isl": side * 2 + lax.rem(core + 1, 2)}
    far = {"isl": lax.rem(side + 1, 2) * 2 + core}

    @pl.when(t == 0)
    def _():
        enter([partner, far])

    def copy_a(slot):
        return pltpu.make_async_remote_copy(
            send_a.at[slot], recv_a.at[slot], sa_sem.at[slot], ra_sem.at[slot],
            device_id=partner, device_id_type=MESH)

    def copy_b(slot):
        return pltpu.make_async_remote_copy(
            send_b.at[slot], recv_b.at[slot], sb_sem.at[slot], rb_sem.at[slot],
            device_id=far, device_id_type=MESH)

    @pl.when(t < chunks)
    def _():
        slot = lax.rem(t, SLOTS)

        @pl.when(t >= SLOTS)
        def _():
            copy_a(slot).wait_send()
            pl.semaphore_wait(credit_a, 1)

        k = t // per
        g0m, g1m = coef_ref[k, 0], coef_ref[k, 1]
        g0v, g1v = coef_ref[k, 2], coef_ref[k, 3]
        eps, factor, hold = coef_ref[k, 4], coef_ref[k, 5], coef_ref[k, 6]
        lhs0, lhs1 = lhs0_ref[0], lhs1_ref[0]
        for role in range(4):
            owner = lax.rem(side + role // 2, 2) * 2 + lax.rem(core + role % 2, 2)
            for start in range(0, quarter, width):
                cols = pl.ds(pl.multiple_of(owner * quarter + start, 128), width)
                g0 = jnp.dot(lhs0, rhs0_ref[0, :, cols], preferred_element_type=jnp.float32)
                g1 = jnp.dot(lhs1, rhs1_ref[0, :, cols], preferred_element_type=jnp.float32)
                first = m_ref[0, :, cols].astype(jnp.float32) + g0m * g0 + g1m * g1
                second = (v_ref[0, :, cols].astype(jnp.float32) + g0v * (g0 * g0)
                          + g1v * (g1 * g1))
                root = second * lax.rsqrt(second) + eps
                term = (hold * p_ref[0, :, cols].astype(jnp.float32)
                        + factor * first / root).astype(jnp.bfloat16)
                if role % 2 == 0:
                    keep[slot, role // 2, :, pl.ds(start, width)] = term
                else:
                    send_a[slot, role // 2, :, pl.ds(start, width)] = term
        copy_a(slot).start()

    @pl.when((t >= 1) & (t < chunks + 1))
    def _():
        chunk = t - 1
        slot = lax.rem(chunk, SLOTS)
        copy_a(slot).wait_recv()

        @pl.when(chunk >= SLOTS)
        def _():
            copy_b(slot).wait_send()
            pl.semaphore_wait(credit_b, 1)

        send_b[slot] = (keep[slot, 1].astype(jnp.float32)
                        + recv_a[slot, 1].astype(jnp.float32)).astype(jnp.bfloat16)
        copy_b(slot).start()
        near[slot] = keep[slot, 0].astype(jnp.float32) + recv_a[slot, 0].astype(jnp.float32)

        @pl.when(chunk + SLOTS < chunks)
        def _():
            pl.semaphore_signal(credit_a, inc=1, device_id=partner, device_id_type=MESH)

    @pl.when(t >= LAG)
    def _():
        chunk = t - LAG
        slot = lax.rem(chunk, SLOTS)
        copy_b(slot).wait_recv()
        weights = w_ref[0]
        delta = (near[slot] + recv_b[slot].astype(jnp.float32)) * 0.25 + coef_ref[0, 7] * weights
        momentum = nesterov_coef * mom_ref[0] + delta
        newm_ref[0] = momentum
        neww_ref[0] = weights - outer_rate * (delta + nesterov_coef * momentum)

        @pl.when(chunk + SLOTS < chunks)
        def _():
            pl.semaphore_signal(credit_b, inc=1, device_id=far, device_id_type=MESH)

    @pl.when(t == chunks + LAG - 1)
    def _():
        for chunk in range(max(chunks - SLOTS, 0), chunks):
            copy_a(chunk % SLOTS).wait_send()
            copy_b(chunk % SLOTS).wait_send()


def last_update(coefs, m, v, p, lhs0, lhs1, rhs0, rhs1, w, mom):
    mats, rows, width = m.shape
    quarter = w.shape[2]
    tokens = lhs0.shape[2]
    tile = next(t for t in (64, 32, 16, 8) if rows % t == 0)
    per = rows // tile
    chunks = mats * per

    def ahead(t):
        t = jnp.minimum(t, chunks - 1)
        return (t // per, lax.rem(t, per), 0)

    def behind(t):
        t = jnp.maximum(t - LAG, 0)
        return (t // per, lax.rem(t, per), 0)

    def side(t):
        return (jnp.minimum(t, chunks - 1) // per // 2, 0, 0)

    wide = pl.BlockSpec((1, tile, width), ahead)
    thin = pl.BlockSpec((1, tile, tokens), ahead)
    rhs = pl.BlockSpec((1, tokens, width), side)
    state = pl.BlockSpec((1, tile, quarter), behind)
    return pl.pallas_call(
        functools.partial(last_kernel, chunks, per, tile, quarter, min(256, quarter)),
        grid=(chunks + LAG,),
        out_shape=(jax.ShapeDtypeStruct(w.shape, jnp.float32),) * 2,
        in_specs=[pl.BlockSpec(memory_space=pltpu.SMEM), wide, wide, wide, thin, thin, rhs, rhs,
                  state, state],
        out_specs=(state, state),
        scratch_shapes=[
            pltpu.VMEM((SLOTS, 2, tile, quarter), jnp.bfloat16),
            pltpu.VMEM((SLOTS, 2, tile, quarter), jnp.bfloat16),
            pltpu.VMEM((SLOTS, 2, tile, quarter), jnp.bfloat16),
            pltpu.VMEM((SLOTS, tile, quarter), jnp.float32),
            pltpu.VMEM((SLOTS, tile, quarter), jnp.bfloat16),
            pltpu.VMEM((SLOTS, tile, quarter), jnp.bfloat16),
            pltpu.SemaphoreType.DMA((SLOTS,)),
            pltpu.SemaphoreType.DMA((SLOTS,)),
            pltpu.SemaphoreType.DMA((SLOTS,)),
            pltpu.SemaphoreType.DMA((SLOTS,)),
            pltpu.SemaphoreType.REGULAR,
            pltpu.SemaphoreType.REGULAR,
        ],
        compiler_params=pltpu.CompilerParams(
            collective_id=2, has_side_effects=True, dimension_semantics=("arbitrary",),
            vmem_limit_bytes=48 << 20),
        name="last_update",
    )(coefs, m, v, p, lhs0, lhs1, rhs0, rhs1, w, mom)


def backward(slopes, hidden, hidden_slope, up_pre, activated, slope):
    gate_slope = (hidden_slope * up_pre * slope).astype(jnp.bfloat16)
    up_slope = (hidden_slope * activated).astype(jnp.bfloat16)
    return jnp.stack([gate_slope.T, up_slope.T, hidden.T])


def body(n_isl, n_fsdp, weights, momentum, first_moment, second_moment, inputs, targets,
         overflow_step):
    moment_one = first_moment[0]
    moment_two = second_moment[0]
    rows = inputs.shape[1]
    width = inputs.shape[2]
    local_hidden = weights.shape[1]
    hidden_units = local_hidden * n_fsdp
    tokens = rows * n_fsdp
    scale_in, scale_out = 1.0 / math.sqrt(width), 1.0 / math.sqrt(hidden_units)

    gathered = lax.all_gather(weights.astype(jnp.bfloat16), "isl", axis=2, tiled=True)
    line = lax.broadcasted_iota(jnp.int32, (8, 128), 0)
    flags = (line == overflow_step[0, 0]).astype(jnp.float32)
    every, counts = gather_inputs(inputs, flags, n_fsdp, n_isl)
    every = every.reshape(2, tokens, width)

    active = (counts[:, :2, 0] < 0.5).astype(jnp.float32)
    act0, act1 = active[0, 0], active[0, 1]
    shrink = inner_rate * decay_rate
    weight_part = jnp.sum(
        shrink * (active[:, 0] + active[:, 1]) - shrink * shrink * active[:, 0] * active[:, 1]
    ) / n_isl
    keep0, keep1 = 1.0 - shrink * act0, 1.0 - shrink * act1
    scales = jnp.array([scale_in, scale_in, scale_out], jnp.float32)
    zeros = jnp.zeros((3,), jnp.float32)
    root_second = math.sqrt(beta_second)
    coefs0 = jnp.stack([
        (1 - beta_first) / beta_first * scales,
        (1 - beta_second) / beta_second * scales * scales,
        zeros + epsilon / root_second,
        zeros + inner_rate * beta_first / root_second * act0,
    ], axis=1)
    one = 1.0 + (beta_first - 1.0) * act0
    two = 1.0 + (beta_second - 1.0) * act0
    root_two = jnp.sqrt(beta_second * two)
    coefs1 = jnp.stack([
        act0 * (1 - beta_first) / one * scales,
        (1 - beta_first) / (beta_first * one) * scales,
        act0 * (1 - beta_second) / two * scales * scales,
        (1 - beta_second) / (beta_second * two) * scales * scales,
        zeros + epsilon / root_two,
        zeros + inner_rate * act1 * beta_first * one / root_two,
        zeros + keep1,
        zeros + weight_part,
    ], axis=1)

    both = every.reshape(2 * tokens, width)
    gate_all = contract_last(both, gathered[0])
    up_all = contract_last(both, gathered[1])

    def down(part):
        return part.astype(jnp.bfloat16).reshape(n_fsdp, rows, width)

    gate_pre, up_pre = gate_all[:tokens] * scale_in, up_all[:tokens] * scale_in
    activated, slope = silu_parts(gate_pre)
    hidden0 = (activated * up_pre).astype(jnp.bfloat16)
    part = jnp.dot(hidden0, gathered[2], preferred_element_type=jnp.float32)
    slopes0 = island_slopes(down(part), inputs[0], targets[0], hidden_units)
    slopes0 = slopes0.reshape(tokens, width)
    hidden_slope = contract_last(slopes0, gathered[2]) * scale_out
    lhs0 = backward(slopes0, hidden0, hidden_slope, up_pre, activated, slope)
    rhs0 = jnp.stack([every[0], slopes0])
    step0 = first_update(coefs0, moment_one, moment_two, lhs0, rhs0)

    gate_pre = (keep0 * gate_all[tokens:] - contract_last(every[1], step0[0])) * scale_in
    up_pre = (keep0 * up_all[tokens:] - contract_last(every[1], step0[1])) * scale_in
    activated, slope = silu_parts(gate_pre)
    hidden1 = (activated * up_pre).astype(jnp.bfloat16)
    part = (keep0 * jnp.dot(hidden1, gathered[2], preferred_element_type=jnp.float32)
            - jnp.dot(hidden1, step0[2], preferred_element_type=jnp.float32))
    slopes1 = island_slopes(down(part), inputs[1], targets[1], hidden_units)
    slopes1 = slopes1.reshape(tokens, width)
    hidden_slope = (keep0 * contract_last(slopes1, gathered[2])
                    - contract_last(slopes1, step0[2])) * scale_out
    lhs1 = backward(slopes1, hidden1, hidden_slope, up_pre, activated, slope)
    rhs1 = jnp.stack([every[1], slopes1])
    return last_update(coefs1, moment_one, moment_two, step0, lhs0, lhs1, rhs0, rhs1,
                       weights, momentum)


def solution(mesh):
    in_specs = (
        P(None, "fsdp", "isl"),
        P(None, "fsdp", "isl"),
        P("isl", None, "fsdp", None),
        P("isl", None, "fsdp", None),
        P(None, ("isl", "fsdp"), None),
        P(None, ("isl", "fsdp"), None),
        P("isl", "fsdp"),
    )
    out_specs = (P(None, "fsdp", "isl"), P(None, "fsdp", "isl"))
    fn = functools.partial(body, mesh.shape["isl"], mesh.shape["fsdp"])
    return jax.shard_map(fn, mesh=mesh, in_specs=in_specs, out_specs=out_specs, check_vma=False)
```

```python
import functools
import math

import jax
import jax.numpy as jnp
from jax import lax
from jax.experimental import pallas as pl
from jax.experimental.pallas import tpu as pltpu
from jax.sharding import PartitionSpec as P

MESH = pl.DeviceIdType.MESH

inner_rate = 0.02
beta_first = 0.9
beta_second = 0.95
epsilon = 1e-08
decay_rate = 0.1
outer_rate = 0.7
nesterov_coef = 0.9


def silu_parts(preact):
    sigmoid_value = jax.nn.sigmoid(preact)
    return (preact * sigmoid_value, sigmoid_value * (1.0 + preact * (1.0 - sigmoid_value)))


def contract_last(left_side, right_side):
    return lax.dot_general(
        left_side, right_side, (((1,), (1,)), ((), ())), preferred_element_type=jnp.float32
    )


def enter(peers):
    barrier = pltpu.get_barrier_semaphore()
    for peer in peers:
        pl.semaphore_signal(barrier, inc=1, device_id=peer, device_id_type=MESH)
    pl.semaphore_wait(barrier, len(peers))


def gather_kernel(n, n_isl, x_ref, flag_ref, out_ref, count_ref, got, flags, counts, own,
                  send_sem, recv_sem, fsend_sem, frecv_sem, csend_sem, crecv_sem):
    isl = lax.axis_index("isl")
    me = lax.axis_index("fsdp")
    enter(
        [{"fsdp": lax.rem(me + d, n)} for d in range(1, n)]
        + [{"isl": lax.rem(isl + d, n_isl)} for d in range(1, n_isl)]
    )
    copies = []
    for d in range(1, n):
        to = {"fsdp": lax.rem(me + d, n)}
        small = pltpu.make_async_remote_copy(
            flag_ref, flags.at[d - 1], fsend_sem.at[d - 1], frecv_sem.at[d - 1],
            device_id=to, device_id_type=MESH)
        small.start()
        big = pltpu.make_async_remote_copy(
            x_ref, got.at[d - 1], send_sem.at[d - 1], recv_sem.at[d - 1],
            device_id=to, device_id_type=MESH)
        big.start()
        copies.append((small, big))
    total = flag_ref[...]
    for d in range(1, n):
        copies[d - 1][0].wait()
        total = total + flags[d - 1]
    own[...] = total
    sent = []
    for d in range(1, n_isl):
        copy = pltpu.make_async_remote_copy(
            own, counts.at[d - 1], csend_sem.at[d - 1], crecv_sem.at[d - 1],
            device_id={"isl": lax.rem(isl + d, n_isl)}, device_id_type=MESH)
        copy.start()
        sent.append(copy)
    count_ref[0] = total
    for k in range(x_ref.shape[0]):
        out_ref[k, me] = x_ref[k]
    for d in range(1, n):
        copies[d - 1][1].wait()
        for k in range(x_ref.shape[0]):
            out_ref[k, lax.rem(me + n - d, n)] = got[d - 1, k]
    for d in range(1, n_isl):
        sent[d - 1].wait()
        count_ref[d] = counts[d - 1]


def gather_inputs(x, flags, n, n_isl):
    steps, rows, width = x.shape
    vmem = pl.BlockSpec(memory_space=pltpu.VMEM)
    return pl.pallas_call(
        functools.partial(gather_kernel, n, n_isl),
        out_shape=(jax.ShapeDtypeStruct((steps, n, rows, width), x.dtype),
                   jax.ShapeDtypeStruct((n_isl, 8, 128), jnp.float32)),
        in_specs=[vmem, vmem],
        out_specs=(vmem, vmem),
        scratch_shapes=[
            pltpu.VMEM((n - 1, steps, rows, width), x.dtype),
            pltpu.VMEM((n - 1, 8, 128), jnp.float32),
            pltpu.VMEM((n_isl - 1, 8, 128), jnp.float32),
            pltpu.VMEM((8, 128), jnp.float32),
            pltpu.SemaphoreType.DMA((n - 1,)),
            pltpu.SemaphoreType.DMA((n - 1,)),
            pltpu.SemaphoreType.DMA((n - 1,)),
            pltpu.SemaphoreType.DMA((n - 1,)),
            pltpu.SemaphoreType.DMA((n_isl - 1,)),
            pltpu.SemaphoreType.DMA((n_isl - 1,)),
        ],
        compiler_params=pltpu.CompilerParams(
            collective_id=0, has_side_effects=True, vmem_limit_bytes=40 << 20),
        name="gather_inputs",
    )(x, flags)


def preact_kernel(x_ref, w_ref, out_ref, w_half, got, keep, send_a, recv_a, send_b, recv_b,
                  sx_sem, rx_sem, sa_sem, ra_sem, sb_sem, rb_sem):
    me = lax.axis_index("isl")
    side, core = me // 2, lax.rem(me, 2)
    index = [lax.rem(side + r // 2, 2) * 2 + lax.rem(core + r % 2, 2) for r in range(4)]
    enter([{"isl": index[r]} for r in (1, 2, 3)])
    moved = {}
    for r in (3, 2, 1):
        moved[r] = pltpu.make_async_remote_copy(
            x_ref.at[index[r]], got.at[r - 1], sx_sem.at[r - 1], rx_sem.at[r - 1],
            device_id={"isl": index[r]}, device_id_type=MESH)
        moved[r].start()
    for half in range(2):
        w_half[half] = w_ref[half].astype(jnp.bfloat16)

    def copy_a(slot):
        return pltpu.make_async_remote_copy(
            send_a.at[slot], recv_a.at[slot], sa_sem.at[slot], ra_sem.at[slot],
            device_id={"isl": index[1]}, device_id_type=MESH)

    def partial(x):
        return [contract_last(x, w_half[half]) for half in range(2)]

    for half, value in enumerate(partial(x_ref[me])):
        out_ref[half] = value
    moved[1].wait()
    for half, value in enumerate(partial(got[0])):
        send_a[0, half] = value.astype(jnp.bfloat16)
    copy_a(0).start()
    moved[3].wait()
    for half, value in enumerate(partial(got[2])):
        send_a[1, half] = value.astype(jnp.bfloat16)
    copy_a(1).start()
    moved[2].wait()
    for half, value in enumerate(partial(got[1])):
        keep[half] = value
    copy_a(1).wait()
    for half in range(2):
        send_b[half] = (keep[half] + recv_a[1, half].astype(jnp.float32)).astype(jnp.bfloat16)
    last = pltpu.make_async_remote_copy(
        send_b, recv_b, sb_sem, rb_sem, device_id={"isl": index[2]}, device_id_type=MESH)
    last.start()
    copy_a(0).wait()
    for half in range(2):
        out_ref[half] = out_ref[half] + recv_a[0, half].astype(jnp.float32)
    last.wait()
    for half in range(2):
        out_ref[half] = out_ref[half] + recv_b[half].astype(jnp.float32)


def preactivations(x, w):
    n_isl, tokens, quarter = x.shape
    rows = w.shape[1]
    vmem = pl.BlockSpec(memory_space=pltpu.VMEM)
    dma = pltpu.SemaphoreType.DMA
    return pl.pallas_call(
        preact_kernel,
        grid=(1,),
        out_shape=jax.ShapeDtypeStruct((2, tokens, rows), jnp.float32),
        in_specs=[pl.BlockSpec((n_isl, tokens, quarter), lambda i: (0, 0, 0)),
                  pl.BlockSpec((2, rows, quarter), lambda i: (0, 0, 0),
                               pipeline_mode=pl.Buffered(1))],
        out_specs=pl.BlockSpec((2, tokens, rows), lambda i: (0, 0, 0)),
        scratch_shapes=[
            pltpu.VMEM((2, rows, quarter), jnp.bfloat16),
            pltpu.VMEM((3, tokens, quarter), jnp.bfloat16),
            pltpu.VMEM((2, tokens, rows), jnp.float32),
            pltpu.VMEM((2, 2, tokens, rows), jnp.bfloat16),
            pltpu.VMEM((2, 2, tokens, rows), jnp.bfloat16),
            pltpu.VMEM((2, tokens, rows), jnp.bfloat16),
            pltpu.VMEM((2, tokens, rows), jnp.bfloat16),
            dma((3,)), dma((3,)), dma((2,)), dma((2,)), dma, dma,
        ],
        compiler_params=pltpu.CompilerParams(
            collective_id=3, has_side_effects=True, dimension_semantics=("arbitrary",),
            vmem_limit_bytes=48 << 20),
        name="preactivations",
    )(x, w)


def slopes_kernel(n, scale, inverse, part_ref, x_ref, y_ref, out_ref, got, own, back,
                  send_sem, recv_sem, send_two, recv_two):
    me = lax.axis_index("fsdp")
    enter([{"fsdp": lax.rem(me + d, n)} for d in range(1, n)])
    copies = []
    for d in range(1, n):
        peer = lax.rem(me + d, n)
        copy = pltpu.make_async_remote_copy(
            part_ref.at[peer], got.at[d - 1], send_sem.at[d - 1], recv_sem.at[d - 1],
            device_id={"fsdp": peer}, device_id_type=MESH)
        copy.start()
        copies.append(copy)
    total = part_ref[me].astype(jnp.float32)
    for d in range(1, n):
        copies[d - 1].wait()
        total = total + got[d - 1].astype(jnp.float32)
    outputs = x_ref[...].astype(jnp.float32) + total * scale
    own[...] = ((outputs - y_ref[...].astype(jnp.float32)) * inverse).astype(jnp.bfloat16)
    copies = []
    for d in range(1, n):
        copy = pltpu.make_async_remote_copy(
            own, back.at[d - 1], send_two.at[d - 1], recv_two.at[d - 1],
            device_id={"fsdp": lax.rem(me + d, n)}, device_id_type=MESH)
        copy.start()
        copies.append(copy)
    out_ref[me] = own[...]
    for d in range(1, n):
        copies[d - 1].wait()
        out_ref[lax.rem(me + n - d, n)] = back[d - 1]


def island_slopes(part, x, y, hidden_units):
    n, rows, width = part.shape
    vmem = pl.BlockSpec(memory_space=pltpu.VMEM)
    return pl.pallas_call(
        functools.partial(
            slopes_kernel, n, 1.0 / math.sqrt(hidden_units), 1.0 / (n * rows)),
        out_shape=jax.ShapeDtypeStruct((n, rows, width), jnp.bfloat16),
        in_specs=[vmem] * 3,
        out_specs=vmem,
        scratch_shapes=[
            pltpu.VMEM((n - 1, rows, width), part.dtype),
            pltpu.VMEM((rows, width), jnp.bfloat16),
            pltpu.VMEM((n - 1, rows, width), jnp.bfloat16),
            pltpu.SemaphoreType.DMA((n - 1,)),
            pltpu.SemaphoreType.DMA((n - 1,)),
            pltpu.SemaphoreType.DMA((n - 1,)),
            pltpu.SemaphoreType.DMA((n - 1,)),
        ],
        compiler_params=pltpu.CompilerParams(
            collective_id=1, has_side_effects=True, vmem_limit_bytes=40 << 20),
        name="island_slopes",
    )(part, x, y)


def first_kernel(width, coef_ref, m_ref, v_ref, lhs_ref, rhs_ref, next_ref, out_ref, pre_ref):
    k = pl.program_id(0)
    grad_m, grad_v = coef_ref[k, 0], coef_ref[k, 1]
    eps, factor = coef_ref[k, 2], coef_ref[k, 3]
    lhs = lhs_ref[0]
    total = jnp.zeros(pre_ref.shape[1:], jnp.float32)
    for start in range(0, m_ref.shape[2], width):
        cols = pl.ds(start, width)
        grad = jnp.dot(lhs, rhs_ref[0, :, cols], preferred_element_type=jnp.float32)
        first = m_ref[0, :, cols].astype(jnp.float32) + grad_m * grad
        second = v_ref[0, :, cols].astype(jnp.float32) + grad_v * (grad * grad)
        root = second * lax.rsqrt(second) + eps
        term = (factor * first / root).astype(jnp.bfloat16)
        out_ref[0, :, cols] = term
        total = total + contract_last(term, next_ref[:, cols])
    pre_ref[0] = total


def first_update(coefs, m, v, lhs, rhs, following):
    mats, rows, width = m.shape
    tokens = lhs.shape[2]
    tile = next(t for t in (128, 64, 32, 16, 8) if rows % t == 0)
    block = pl.BlockSpec((1, tile, width), lambda k, r: (k, r, 0))
    return pl.pallas_call(
        functools.partial(first_kernel, min(256, width)),
        grid=(mats, rows // tile),
        out_shape=(jax.ShapeDtypeStruct(m.shape, jnp.bfloat16),
                   jax.ShapeDtypeStruct(lhs.shape, jnp.float32)),
        in_specs=[
            pl.BlockSpec(memory_space=pltpu.SMEM),
            block,
            block,
            pl.BlockSpec((1, tile, tokens), lambda k, r: (k, r, 0)),
            pl.BlockSpec((1, tokens, width), lambda k, r: (k // 2, 0, 0)),
            pl.BlockSpec((tokens, width), lambda k, r: (0, 0)),
        ],
        out_specs=(block, pl.BlockSpec((1, tile, tokens), lambda k, r: (k, r, 0))),
        compiler_params=pltpu.CompilerParams(
            dimension_semantics=("arbitrary", "arbitrary"), vmem_limit_bytes=40 << 20),
        name="first_update",
    )(coefs, m, v, lhs, rhs, following)


SLOTS = 8
LAG = 4


def last_kernel(chunks, per, tile, quarter, width, coef_ref, m_ref, v_ref, p_ref, lhs0_ref,
                lhs1_ref, rhs0_ref, rhs1_ref, w_ref, mom_ref, neww_ref, newm_ref,
                keep, send_a, recv_a, near, send_b, recv_b,
                sa_sem, ra_sem, sb_sem, rb_sem, credit_a, credit_b):
    t = pl.program_id(0)
    me = lax.axis_index("isl")
    side, core = me // 2, lax.rem(me, 2)
    partner = {"isl": side * 2 + lax.rem(core + 1, 2)}
    far = {"isl": lax.rem(side + 1, 2) * 2 + core}

    @pl.when(t == 0)
    def _():
        enter([partner, far])

    def copy_a(slot):
        return pltpu.make_async_remote_copy(
            send_a.at[slot], recv_a.at[slot], sa_sem.at[slot], ra_sem.at[slot],
            device_id=partner, device_id_type=MESH)

    def copy_b(slot):
        return pltpu.make_async_remote_copy(
            send_b.at[slot], recv_b.at[slot], sb_sem.at[slot], rb_sem.at[slot],
            device_id=far, device_id_type=MESH)

    @pl.when(t < chunks)
    def _():
        slot = lax.rem(t, SLOTS)

        @pl.when(t >= SLOTS)
        def _():
            copy_a(slot).wait_send()
            pl.semaphore_wait(credit_a, 1)

        k = t // per
        g0m, g1m = coef_ref[k, 0], coef_ref[k, 1]
        g0v, g1v = coef_ref[k, 2], coef_ref[k, 3]
        eps, factor, hold = coef_ref[k, 4], coef_ref[k, 5], coef_ref[k, 6]
        lhs0, lhs1 = lhs0_ref[0], lhs1_ref[0]
        for role in range(4):
            owner = lax.rem(side + role // 2, 2) * 2 + lax.rem(core + role % 2, 2)
            for start in range(0, quarter, width):
                cols = pl.ds(pl.multiple_of(owner * quarter + start, 128), width)
                g0 = jnp.dot(lhs0, rhs0_ref[0, :, cols], preferred_element_type=jnp.float32)
                g1 = jnp.dot(lhs1, rhs1_ref[0, :, cols], preferred_element_type=jnp.float32)
                first = m_ref[0, :, cols].astype(jnp.float32) + g0m * g0 + g1m * g1
                second = (v_ref[0, :, cols].astype(jnp.float32) + g0v * (g0 * g0)
                          + g1v * (g1 * g1))
                root = second * lax.rsqrt(second) + eps
                term = (hold * p_ref[0, :, cols].astype(jnp.float32)
                        + factor * first / root).astype(jnp.bfloat16)
                if role % 2 == 0:
                    keep[slot, role // 2, :, pl.ds(start, width)] = term
                else:
                    send_a[slot, role // 2, :, pl.ds(start, width)] = term
        copy_a(slot).start()

    @pl.when((t >= 1) & (t < chunks + 1))
    def _():
        chunk = t - 1
        slot = lax.rem(chunk, SLOTS)
        copy_a(slot).wait_recv()

        @pl.when(chunk >= SLOTS)
        def _():
            copy_b(slot).wait_send()
            pl.semaphore_wait(credit_b, 1)

        send_b[slot] = (keep[slot, 1].astype(jnp.float32)
                        + recv_a[slot, 1].astype(jnp.float32)).astype(jnp.bfloat16)
        copy_b(slot).start()
        near[slot] = keep[slot, 0].astype(jnp.float32) + recv_a[slot, 0].astype(jnp.float32)

        @pl.when(chunk + SLOTS < chunks)
        def _():
            pl.semaphore_signal(credit_a, inc=1, device_id=partner, device_id_type=MESH)

    @pl.when(t >= LAG)
    def _():
        chunk = t - LAG
        slot = lax.rem(chunk, SLOTS)
        copy_b(slot).wait_recv()
        weights = w_ref[0]
        delta = (near[slot] + recv_b[slot].astype(jnp.float32)) * 0.25 + coef_ref[0, 7] * weights
        momentum = nesterov_coef * mom_ref[0] + delta
        newm_ref[0] = momentum
        neww_ref[0] = weights - outer_rate * (delta + nesterov_coef * momentum)

        @pl.when(chunk + SLOTS < chunks)
        def _():
            pl.semaphore_signal(credit_b, inc=1, device_id=far, device_id_type=MESH)

    @pl.when(t == chunks + LAG - 1)
    def _():
        for chunk in range(max(chunks - SLOTS, 0), chunks):
            copy_a(chunk % SLOTS).wait_send()
            copy_b(chunk % SLOTS).wait_send()


def last_update(coefs, m, v, p, lhs0, lhs1, rhs0, rhs1, w, mom):
    mats, rows, width = m.shape
    quarter = w.shape[2]
    tokens = lhs0.shape[2]
    tile = next(t for t in (64, 32, 16, 8) if rows % t == 0)
    per = rows // tile
    chunks = mats * per

    def ahead(t):
        t = jnp.minimum(t, chunks - 1)
        return (t // per, lax.rem(t, per), 0)

    def behind(t):
        t = jnp.maximum(t - LAG, 0)
        return (t // per, lax.rem(t, per), 0)

    def side(t):
        return (jnp.minimum(t, chunks - 1) // per // 2, 0, 0)

    wide = pl.BlockSpec((1, tile, width), ahead)
    thin = pl.BlockSpec((1, tile, tokens), ahead)
    rhs = pl.BlockSpec((1, tokens, width), side)
    state = pl.BlockSpec((1, tile, quarter), behind)
    return pl.pallas_call(
        functools.partial(last_kernel, chunks, per, tile, quarter, min(256, quarter)),
        grid=(chunks + LAG,),
        out_shape=(jax.ShapeDtypeStruct(w.shape, jnp.float32),) * 2,
        in_specs=[pl.BlockSpec(memory_space=pltpu.SMEM), wide, wide, wide, thin, thin, rhs, rhs,
                  state, state],
        out_specs=(state, state),
        scratch_shapes=[
            pltpu.VMEM((SLOTS, 2, tile, quarter), jnp.bfloat16),
            pltpu.VMEM((SLOTS, 2, tile, quarter), jnp.bfloat16),
            pltpu.VMEM((SLOTS, 2, tile, quarter), jnp.bfloat16),
            pltpu.VMEM((SLOTS, tile, quarter), jnp.float32),
            pltpu.VMEM((SLOTS, tile, quarter), jnp.bfloat16),
            pltpu.VMEM((SLOTS, tile, quarter), jnp.bfloat16),
            pltpu.SemaphoreType.DMA((SLOTS,)),
            pltpu.SemaphoreType.DMA((SLOTS,)),
            pltpu.SemaphoreType.DMA((SLOTS,)),
            pltpu.SemaphoreType.DMA((SLOTS,)),
            pltpu.SemaphoreType.REGULAR,
            pltpu.SemaphoreType.REGULAR,
        ],
        compiler_params=pltpu.CompilerParams(
            collective_id=2, has_side_effects=True, dimension_semantics=("arbitrary",),
            vmem_limit_bytes=48 << 20),
        name="last_update",
    )(coefs, m, v, p, lhs0, lhs1, rhs0, rhs1, w, mom)


def backward(slopes, hidden, hidden_slope, up_pre, activated, slope):
    gate_slope = (hidden_slope * up_pre * slope).astype(jnp.bfloat16)
    up_slope = (hidden_slope * activated).astype(jnp.bfloat16)
    return jnp.stack([gate_slope.T, up_slope.T, hidden.T])


def body(n_isl, n_fsdp, weights, momentum, first_moment, second_moment, inputs, targets,
         overflow_step):
    moment_one = first_moment[0]
    moment_two = second_moment[0]
    rows = inputs.shape[1]
    width = inputs.shape[2]
    local_hidden = weights.shape[1]
    hidden_units = local_hidden * n_fsdp
    tokens = rows * n_fsdp
    scale_in, scale_out = 1.0 / math.sqrt(width), 1.0 / math.sqrt(hidden_units)

    down_weights = lax.all_gather(weights[2].astype(jnp.bfloat16), "isl", axis=1, tiled=True)
    line = lax.broadcasted_iota(jnp.int32, (8, 128), 0)
    flags = (line == overflow_step[0, 0]).astype(jnp.float32)
    every, counts = gather_inputs(inputs, flags, n_fsdp, n_isl)
    every = every.reshape(2, tokens, width)

    active = (counts[:, :2, 0] < 0.5).astype(jnp.float32)
    act0, act1 = active[0, 0], active[0, 1]
    shrink = inner_rate * decay_rate
    weight_part = jnp.sum(
        shrink * (active[:, 0] + active[:, 1]) - shrink * shrink * active[:, 0] * active[:, 1]
    ) / n_isl
    keep0, keep1 = 1.0 - shrink * act0, 1.0 - shrink * act1
    scales = jnp.array([scale_in, scale_in, scale_out], jnp.float32)
    zeros = jnp.zeros((3,), jnp.float32)
    root_second = math.sqrt(beta_second)
    coefs0 = jnp.stack([
        (1 - beta_first) / beta_first * scales,
        (1 - beta_second) / beta_second * scales * scales,
        zeros + epsilon / root_second,
        zeros + inner_rate * beta_first / root_second * act0,
    ], axis=1)
    one = 1.0 + (beta_first - 1.0) * act0
    two = 1.0 + (beta_second - 1.0) * act0
    root_two = jnp.sqrt(beta_second * two)
    coefs1 = jnp.stack([
        act0 * (1 - beta_first) / one * scales,
        (1 - beta_first) / (beta_first * one) * scales,
        act0 * (1 - beta_second) / two * scales * scales,
        (1 - beta_second) / (beta_second * two) * scales * scales,
        zeros + epsilon / root_two,
        zeros + inner_rate * act1 * beta_first * one / root_two,
        zeros + keep1,
        zeros + weight_part,
    ], axis=1)

    both = every.reshape(2 * tokens, width)
    by_owner = both.reshape(2 * tokens, n_isl, width // n_isl).transpose(1, 0, 2)
    gate_all, up_all = preactivations(by_owner, weights)

    def down(part):
        return part.astype(jnp.bfloat16).reshape(n_fsdp, rows, width)

    gate_pre, up_pre = gate_all[:tokens] * scale_in, up_all[:tokens] * scale_in
    activated, slope = silu_parts(gate_pre)
    hidden0 = (activated * up_pre).astype(jnp.bfloat16)
    part = jnp.dot(hidden0, down_weights, preferred_element_type=jnp.float32)
    slopes0 = island_slopes(down(part), inputs[0], targets[0], hidden_units)
    slopes0 = slopes0.reshape(tokens, width)
    hidden_slope = contract_last(slopes0, down_weights) * scale_out
    lhs0 = backward(slopes0, hidden0, hidden_slope, up_pre, activated, slope)
    rhs0 = jnp.stack([every[0], slopes0])
    step0, moved = first_update(coefs0, moment_one, moment_two, lhs0, rhs0, every[1])

    gate_pre = (keep0 * gate_all[tokens:] - moved[0].T) * scale_in
    up_pre = (keep0 * up_all[tokens:] - moved[1].T) * scale_in
    activated, slope = silu_parts(gate_pre)
    hidden1 = (activated * up_pre).astype(jnp.bfloat16)
    part = (keep0 * jnp.dot(hidden1, down_weights, preferred_element_type=jnp.float32)
            - jnp.dot(hidden1, step0[2], preferred_element_type=jnp.float32))
    slopes1 = island_slopes(down(part), inputs[1], targets[1], hidden_units)
    slopes1 = slopes1.reshape(tokens, width)
    hidden_slope = (keep0 * contract_last(slopes1, down_weights)
                    - contract_last(slopes1, step0[2])) * scale_out
    lhs1 = backward(slopes1, hidden1, hidden_slope, up_pre, activated, slope)
    rhs1 = jnp.stack([every[1], slopes1])
    return last_update(coefs1, moment_one, moment_two, step0, lhs0, lhs1, rhs0, rhs1,
                       weights, momentum)


def solution(mesh):
    in_specs = (
        P(None, "fsdp", "isl"),
        P(None, "fsdp", "isl"),
        P("isl", None, "fsdp", None),
        P("isl", None, "fsdp", None),
        P(None, ("isl", "fsdp"), None),
        P(None, ("isl", "fsdp"), None),
        P("isl", "fsdp"),
    )
    out_specs = (P(None, "fsdp", "isl"), P(None, "fsdp", "isl"))
    fn = functools.partial(body, mesh.shape["isl"], mesh.shape["fsdp"])
    return jax.shard_map(fn, mesh=mesh, in_specs=in_specs, out_specs=out_specs, check_vma=False)
```

```python
import functools
import math

import jax
import jax.numpy as jnp
from jax import lax
from jax.experimental import pallas as pl
from jax.experimental.pallas import tpu as pltpu
from jax.sharding import PartitionSpec as P

MESH = pl.DeviceIdType.MESH

inner_rate = 0.02
beta_first = 0.9
beta_second = 0.95
epsilon = 1e-08
decay_rate = 0.1
outer_rate = 0.7
nesterov_coef = 0.9


def silu_parts(preact):
    sigmoid_value = jax.nn.sigmoid(preact)
    return (preact * sigmoid_value, sigmoid_value * (1.0 + preact * (1.0 - sigmoid_value)))


def contract_last(left_side, right_side):
    return lax.dot_general(
        left_side, right_side, (((1,), (1,)), ((), ())), preferred_element_type=jnp.float32
    )


def enter(peers):
    barrier = pltpu.get_barrier_semaphore()
    for peer in peers:
        pl.semaphore_signal(barrier, inc=1, device_id=peer, device_id_type=MESH)
    pl.semaphore_wait(barrier, len(peers))


def ring_of(me, n):
    pair = me // 2 * 2 + lax.rem(me + 1, 2)
    return pair, [lax.rem(me + 2 * d, n) for d in range(n // 2)]


def spread(me, n, src, got_pair, got_ring, pair_send, pair_recv, ring_send, ring_recv):
    pair, ring = ring_of(me, n)

    def to_pair(block, d):
        return pltpu.make_async_remote_copy(
            block, got_pair.at[d], pair_send.at[d], pair_recv.at[d],
            device_id={"fsdp": pair}, device_id_type=MESH)

    def to_ring(d):
        return pltpu.make_async_remote_copy(
            src, got_ring.at[d - 1], ring_send.at[d - 1], ring_recv.at[d - 1],
            device_id={"fsdp": ring[d]}, device_id_type=MESH)

    around = [to_ring(d) for d in range(1, n // 2)]
    for copy in around:
        copy.start()
    across = [to_pair(src, 0)]
    across[0].start()

    def arrivals():
        for d in range(1, n // 2):
            around[d - 1].wait_recv()
            across.append(to_pair(got_ring.at[d - 1], d))
            across[d].start()
            yield lax.rem(me + n - 2 * d, n), got_ring.at[d - 1]
        for d in range(n // 2):
            across[d].wait_recv()
            yield lax.rem(pair + n - 2 * d, n), got_pair.at[d]
        for copy in around + across:
            copy.wait_send()

    return arrivals


def gather_kernel(n, n_isl, x_ref, flag_ref, out_ref, count_ref, got_pair, got_ring, flags,
                  counts, own, pair_send, pair_recv, ring_send, ring_recv,
                  fsend_sem, frecv_sem, csend_sem, crecv_sem):
    isl = lax.axis_index("isl")
    me = lax.axis_index("fsdp")
    enter(
        [{"fsdp": lax.rem(me + d, n)} for d in range(1, n)]
        + [{"isl": lax.rem(isl + d, n_isl)} for d in range(1, n_isl)]
    )
    small = []
    for d in range(1, n):
        copy = pltpu.make_async_remote_copy(
            flag_ref, flags.at[d - 1], fsend_sem.at[d - 1], frecv_sem.at[d - 1],
            device_id={"fsdp": lax.rem(me + d, n)}, device_id_type=MESH)
        copy.start()
        small.append(copy)
    arrivals = spread(me, n, x_ref, got_pair, got_ring, pair_send, pair_recv, ring_send,
                      ring_recv)
    total = flag_ref[...]
    for d in range(1, n):
        small[d - 1].wait()
        total = total + flags[d - 1]
    own[...] = total
    sent = []
    for d in range(1, n_isl):
        copy = pltpu.make_async_remote_copy(
            own, counts.at[d - 1], csend_sem.at[d - 1], crecv_sem.at[d - 1],
            device_id={"isl": lax.rem(isl + d, n_isl)}, device_id_type=MESH)
        copy.start()
        sent.append(copy)
    count_ref[0] = total
    for k in range(x_ref.shape[0]):
        out_ref[k, me] = x_ref[k]
    for device, block in arrivals():
        for k in range(x_ref.shape[0]):
            out_ref[k, device] = block[k]
    for d in range(1, n_isl):
        sent[d - 1].wait()
        count_ref[d] = counts[d - 1]


def gather_inputs(x, flags, n, n_isl):
    steps, rows, width = x.shape
    vmem = pl.BlockSpec(memory_space=pltpu.VMEM)
    return pl.pallas_call(
        functools.partial(gather_kernel, n, n_isl),
        out_shape=(jax.ShapeDtypeStruct((steps, n, rows, width), x.dtype),
                   jax.ShapeDtypeStruct((n_isl, 8, 128), jnp.float32)),
        in_specs=[vmem, vmem],
        out_specs=(vmem, vmem),
        scratch_shapes=[
            pltpu.VMEM((n // 2, steps, rows, width), x.dtype),
            pltpu.VMEM((n // 2, steps, rows, width), x.dtype),
            pltpu.VMEM((n - 1, 8, 128), jnp.float32),
            pltpu.VMEM((n_isl - 1, 8, 128), jnp.float32),
            pltpu.VMEM((8, 128), jnp.float32),
        ] + [pltpu.SemaphoreType.DMA((n // 2,))] * 4 + [
            pltpu.SemaphoreType.DMA((n - 1,)),
            pltpu.SemaphoreType.DMA((n - 1,)),
            pltpu.SemaphoreType.DMA((n_isl - 1,)),
            pltpu.SemaphoreType.DMA((n_isl - 1,)),
        ],
        compiler_params=pltpu.CompilerParams(
            collective_id=0, has_side_effects=True, vmem_limit_bytes=40 << 20),
        name="gather_inputs",
    )(x, flags)


def preact_kernel(x_ref, w_ref, out_ref, w_half, got, keep, send_a, recv_a, send_b, recv_b,
                  sx_sem, rx_sem, sa_sem, ra_sem, sb_sem, rb_sem):
    me = lax.axis_index("isl")
    side, core = me // 2, lax.rem(me, 2)
    index = [lax.rem(side + r // 2, 2) * 2 + lax.rem(core + r % 2, 2) for r in range(4)]
    enter([{"isl": index[r]} for r in (1, 2, 3)])
    moved = {}
    for r in (3, 2, 1):
        moved[r] = pltpu.make_async_remote_copy(
            x_ref.at[index[r]], got.at[r - 1], sx_sem.at[r - 1], rx_sem.at[r - 1],
            device_id={"isl": index[r]}, device_id_type=MESH)
        moved[r].start()
    for half in range(2):
        w_half[half] = w_ref[half].astype(jnp.bfloat16)

    def copy_a(slot):
        return pltpu.make_async_remote_copy(
            send_a.at[slot], recv_a.at[slot], sa_sem.at[slot], ra_sem.at[slot],
            device_id={"isl": index[1]}, device_id_type=MESH)

    def partial(x):
        return [contract_last(x, w_half[half]) for half in range(2)]

    for half, value in enumerate(partial(x_ref[me])):
        out_ref[half] = value
    moved[1].wait()
    for half, value in enumerate(partial(got[0])):
        send_a[0, half] = value.astype(jnp.bfloat16)
    copy_a(0).start()
    moved[3].wait()
    for half, value in enumerate(partial(got[2])):
        send_a[1, half] = value.astype(jnp.bfloat16)
    copy_a(1).start()
    moved[2].wait()
    for half, value in enumerate(partial(got[1])):
        keep[half] = value
    copy_a(1).wait()
    for half in range(2):
        send_b[half] = (keep[half] + recv_a[1, half].astype(jnp.float32)).astype(jnp.bfloat16)
    last = pltpu.make_async_remote_copy(
        send_b, recv_b, sb_sem, rb_sem, device_id={"isl": index[2]}, device_id_type=MESH)
    last.start()
    copy_a(0).wait()
    for half in range(2):
        out_ref[half] = out_ref[half] + recv_a[0, half].astype(jnp.float32)
    last.wait()
    for half in range(2):
        out_ref[half] = out_ref[half] + recv_b[half].astype(jnp.float32)


def preactivations(x, w):
    n_isl, tokens, quarter = x.shape
    rows = w.shape[1]
    vmem = pl.BlockSpec(memory_space=pltpu.VMEM)
    dma = pltpu.SemaphoreType.DMA
    return pl.pallas_call(
        preact_kernel,
        grid=(1,),
        out_shape=jax.ShapeDtypeStruct((2, tokens, rows), jnp.float32),
        in_specs=[pl.BlockSpec((n_isl, tokens, quarter), lambda i: (0, 0, 0)),
                  pl.BlockSpec((2, rows, quarter), lambda i: (0, 0, 0),
                               pipeline_mode=pl.Buffered(1))],
        out_specs=pl.BlockSpec((2, tokens, rows), lambda i: (0, 0, 0)),
        scratch_shapes=[
            pltpu.VMEM((2, rows, quarter), jnp.bfloat16),
            pltpu.VMEM((3, tokens, quarter), jnp.bfloat16),
            pltpu.VMEM((2, tokens, rows), jnp.float32),
            pltpu.VMEM((2, 2, tokens, rows), jnp.bfloat16),
            pltpu.VMEM((2, 2, tokens, rows), jnp.bfloat16),
            pltpu.VMEM((2, tokens, rows), jnp.bfloat16),
            pltpu.VMEM((2, tokens, rows), jnp.bfloat16),
            dma((3,)), dma((3,)), dma((2,)), dma((2,)), dma, dma,
        ],
        compiler_params=pltpu.CompilerParams(
            collective_id=3, has_side_effects=True, dimension_semantics=("arbitrary",),
            vmem_limit_bytes=48 << 20),
        name="preactivations",
    )(x, w)


def slopes_kernel(n, scale, inverse, part_ref, x_ref, y_ref, out_ref, got_one, sums, got_two,
                  own, got_pair, got_ring, one_send, one_recv, two_send, two_recv,
                  pair_send, pair_recv, ring_send, ring_recv):
    me = lax.axis_index("fsdp")
    pair, ring = ring_of(me, n)
    half = n // 2
    enter([{"fsdp": pair}] + [{"fsdp": ring[d]} for d in range(1, half)])
    across = {}
    for d in list(range(1, half)) + [0]:
        across[d] = pltpu.make_async_remote_copy(
            part_ref.at[lax.rem(pair + 2 * d, n)], got_one.at[d], one_send.at[d],
            one_recv.at[d], device_id={"fsdp": pair}, device_id_type=MESH)
        across[d].start()
    around = {}
    for d in range(1, half):
        across[d].wait()
        sums[d - 1] = (part_ref[ring[d]].astype(jnp.float32)
                       + got_one[d].astype(jnp.float32)).astype(sums.dtype)
        around[d] = pltpu.make_async_remote_copy(
            sums.at[d - 1], got_two.at[d - 1], two_send.at[d - 1], two_recv.at[d - 1],
            device_id={"fsdp": ring[d]}, device_id_type=MESH)
        around[d].start()
    across[0].wait()
    total = part_ref[me].astype(jnp.float32) + got_one[0].astype(jnp.float32)
    for d in range(1, half):
        around[d].wait()
        total = total + got_two[d - 1].astype(jnp.float32)
    outputs = x_ref[...].astype(jnp.float32) + total * scale
    own[...] = ((outputs - y_ref[...].astype(jnp.float32)) * inverse).astype(jnp.bfloat16)
    arrivals = spread(me, n, own, got_pair, got_ring, pair_send, pair_recv, ring_send,
                      ring_recv)
    out_ref[me] = own[...]
    for device, block in arrivals():
        out_ref[device] = block[...]


def island_slopes(part, x, y, hidden_units):
    n, rows, width = part.shape
    vmem = pl.BlockSpec(memory_space=pltpu.VMEM)
    return pl.pallas_call(
        functools.partial(
            slopes_kernel, n, 1.0 / math.sqrt(hidden_units), 1.0 / (n * rows)),
        out_shape=jax.ShapeDtypeStruct((n, rows, width), jnp.bfloat16),
        in_specs=[vmem] * 3,
        out_specs=vmem,
        scratch_shapes=[
            pltpu.VMEM((n // 2, rows, width), part.dtype),
            pltpu.VMEM((n // 2, rows, width), part.dtype),
            pltpu.VMEM((n // 2, rows, width), part.dtype),
            pltpu.VMEM((rows, width), jnp.bfloat16),
            pltpu.VMEM((n // 2, rows, width), jnp.bfloat16),
            pltpu.VMEM((n // 2, rows, width), jnp.bfloat16),
        ] + [pltpu.SemaphoreType.DMA((n // 2,))] * 8,
        compiler_params=pltpu.CompilerParams(
            collective_id=1, has_side_effects=True, vmem_limit_bytes=40 << 20),
        name="island_slopes",
    )(part, x, y)


def first_kernel(width, coef_ref, m_ref, v_ref, lhs_ref, rhs_ref, next_ref, out_ref, pre_ref):
    k = pl.program_id(0)
    grad_m, grad_v = coef_ref[k, 0], coef_ref[k, 1]
    eps, factor = coef_ref[k, 2], coef_ref[k, 3]
    lhs = lhs_ref[0]
    total = jnp.zeros(pre_ref.shape[1:], jnp.float32)
    for start in range(0, m_ref.shape[2], width):
        cols = pl.ds(start, width)
        grad = jnp.dot(lhs, rhs_ref[0, :, cols], preferred_element_type=jnp.float32)
        first = m_ref[0, :, cols].astype(jnp.float32) + grad_m * grad
        second = v_ref[0, :, cols].astype(jnp.float32) + grad_v * (grad * grad)
        root = second * lax.rsqrt(second) + eps
        term = (factor * first / root).astype(jnp.bfloat16)
        out_ref[0, :, cols] = term
        total = total + contract_last(term, next_ref[:, cols])
    pre_ref[0] = total


def first_update(coefs, m, v, lhs, rhs, following):
    mats, rows, width = m.shape
    tokens = lhs.shape[2]
    tile = next(t for t in (128, 64, 32, 16, 8) if rows % t == 0)
    block = pl.BlockSpec((1, tile, width), lambda k, r: (k, r, 0))
    return pl.pallas_call(
        functools.partial(first_kernel, min(256, width)),
        grid=(mats, rows // tile),
        out_shape=(jax.ShapeDtypeStruct(m.shape, jnp.bfloat16),
                   jax.ShapeDtypeStruct(lhs.shape, jnp.float32)),
        in_specs=[
            pl.BlockSpec(memory_space=pltpu.SMEM),
            block,
            block,
            pl.BlockSpec((1, tile, tokens), lambda k, r: (k, r, 0)),
            pl.BlockSpec((1, tokens, width), lambda k, r: (k // 2, 0, 0)),
            pl.BlockSpec((tokens, width), lambda k, r: (0, 0)),
        ],
        out_specs=(block, pl.BlockSpec((1, tile, tokens), lambda k, r: (k, r, 0))),
        compiler_params=pltpu.CompilerParams(
            dimension_semantics=("arbitrary", "arbitrary"), vmem_limit_bytes=40 << 20),
        name="first_update",
    )(coefs, m, v, lhs, rhs, following)


SLOTS = 8
LAG = 4


def last_kernel(chunks, per, tile, quarter, width, coef_ref, m_ref, v_ref, p_ref, lhs0_ref,
                lhs1_ref, rhs0_ref, rhs1_ref, w_ref, mom_ref, neww_ref, newm_ref,
                keep, send_a, recv_a, near, send_b, recv_b,
                sa_sem, ra_sem, sb_sem, rb_sem, credit_a, credit_b):
    t = pl.program_id(0)
    me = lax.axis_index("isl")
    side, core = me // 2, lax.rem(me, 2)
    partner = {"isl": side * 2 + lax.rem(core + 1, 2)}
    far = {"isl": lax.rem(side + 1, 2) * 2 + core}

    @pl.when(t == 0)
    def _():
        enter([partner, far])

    def copy_a(slot):
        return pltpu.make_async_remote_copy(
            send_a.at[slot], recv_a.at[slot], sa_sem.at[slot], ra_sem.at[slot],
            device_id=partner, device_id_type=MESH)

    def copy_b(slot):
        return pltpu.make_async_remote_copy(
            send_b.at[slot], recv_b.at[slot], sb_sem.at[slot], rb_sem.at[slot],
            device_id=far, device_id_type=MESH)

    @pl.when(t < chunks)
    def _():
        slot = lax.rem(t, SLOTS)

        @pl.when(t >= SLOTS)
        def _():
            copy_a(slot).wait_send()
            pl.semaphore_wait(credit_a, 1)

        k = t // per
        g0m, g1m = coef_ref[k, 0], coef_ref[k, 1]
        g0v, g1v = coef_ref[k, 2], coef_ref[k, 3]
        eps, factor, hold = coef_ref[k, 4], coef_ref[k, 5], coef_ref[k, 6]
        lhs0, lhs1 = lhs0_ref[0], lhs1_ref[0]
        for role in range(4):
            owner = lax.rem(side + role // 2, 2) * 2 + lax.rem(core + role % 2, 2)
            for start in range(0, quarter, width):
                cols = pl.ds(pl.multiple_of(owner * quarter + start, 128), width)
                g0 = jnp.dot(lhs0, rhs0_ref[0, :, cols], preferred_element_type=jnp.float32)
                g1 = jnp.dot(lhs1, rhs1_ref[0, :, cols], preferred_element_type=jnp.float32)
                first = m_ref[0, :, cols].astype(jnp.float32) + g0m * g0 + g1m * g1
                second = (v_ref[0, :, cols].astype(jnp.float32) + g0v * (g0 * g0)
                          + g1v * (g1 * g1))
                root = second * lax.rsqrt(second) + eps
                term = (hold * p_ref[0, :, cols].astype(jnp.float32)
                        + factor * first / root).astype(jnp.bfloat16)
                if role % 2 == 0:
                    keep[slot, role // 2, :, pl.ds(start, width)] = term
                else:
                    send_a[slot, role // 2, :, pl.ds(start, width)] = term
        copy_a(slot).start()

    @pl.when((t >= 1) & (t < chunks + 1))
    def _():
        chunk = t - 1
        slot = lax.rem(chunk, SLOTS)
        copy_a(slot).wait_recv()

        @pl.when(chunk >= SLOTS)
        def _():
            copy_b(slot).wait_send()
            pl.semaphore_wait(credit_b, 1)

        send_b[slot] = (keep[slot, 1].astype(jnp.float32)
                        + recv_a[slot, 1].astype(jnp.float32)).astype(jnp.bfloat16)
        copy_b(slot).start()
        near[slot] = keep[slot, 0].astype(jnp.float32) + recv_a[slot, 0].astype(jnp.float32)

        @pl.when(chunk + SLOTS < chunks)
        def _():
            pl.semaphore_signal(credit_a, inc=1, device_id=partner, device_id_type=MESH)

    @pl.when(t >= LAG)
    def _():
        chunk = t - LAG
        slot = lax.rem(chunk, SLOTS)
        copy_b(slot).wait_recv()
        weights = w_ref[0]
        delta = (near[slot] + recv_b[slot].astype(jnp.float32)) * 0.25 + coef_ref[0, 7] * weights
        momentum = nesterov_coef * mom_ref[0] + delta
        newm_ref[0] = momentum
        neww_ref[0] = weights - outer_rate * (delta + nesterov_coef * momentum)

        @pl.when(chunk + SLOTS < chunks)
        def _():
            pl.semaphore_signal(credit_b, inc=1, device_id=far, device_id_type=MESH)

    @pl.when(t == chunks + LAG - 1)
    def _():
        for chunk in range(max(chunks - SLOTS, 0), chunks):
            copy_a(chunk % SLOTS).wait_send()
            copy_b(chunk % SLOTS).wait_send()


def last_update(coefs, m, v, p, lhs0, lhs1, rhs0, rhs1, w, mom):
    mats, rows, width = m.shape
    quarter = w.shape[2]
    tokens = lhs0.shape[2]
    tile = next(t for t in (64, 32, 16, 8) if rows % t == 0)
    per = rows // tile
    chunks = mats * per

    def ahead(t):
        t = jnp.minimum(t, chunks - 1)
        return (t // per, lax.rem(t, per), 0)

    def behind(t):
        t = jnp.maximum(t - LAG, 0)
        return (t // per, lax.rem(t, per), 0)

    def side(t):
        return (jnp.minimum(t, chunks - 1) // per // 2, 0, 0)

    wide = pl.BlockSpec((1, tile, width), ahead)
    thin = pl.BlockSpec((1, tile, tokens), ahead)
    rhs = pl.BlockSpec((1, tokens, width), side)
    state = pl.BlockSpec((1, tile, quarter), behind)
    return pl.pallas_call(
        functools.partial(last_kernel, chunks, per, tile, quarter, min(256, quarter)),
        grid=(chunks + LAG,),
        out_shape=(jax.ShapeDtypeStruct(w.shape, jnp.float32),) * 2,
        in_specs=[pl.BlockSpec(memory_space=pltpu.SMEM), wide, wide, wide, thin, thin, rhs, rhs,
                  state, state],
        out_specs=(state, state),
        scratch_shapes=[
            pltpu.VMEM((SLOTS, 2, tile, quarter), jnp.bfloat16),
            pltpu.VMEM((SLOTS, 2, tile, quarter), jnp.bfloat16),
            pltpu.VMEM((SLOTS, 2, tile, quarter), jnp.bfloat16),
            pltpu.VMEM((SLOTS, tile, quarter), jnp.float32),
            pltpu.VMEM((SLOTS, tile, quarter), jnp.bfloat16),
            pltpu.VMEM((SLOTS, tile, quarter), jnp.bfloat16),
            pltpu.SemaphoreType.DMA((SLOTS,)),
            pltpu.SemaphoreType.DMA((SLOTS,)),
            pltpu.SemaphoreType.DMA((SLOTS,)),
            pltpu.SemaphoreType.DMA((SLOTS,)),
            pltpu.SemaphoreType.REGULAR,
            pltpu.SemaphoreType.REGULAR,
        ],
        compiler_params=pltpu.CompilerParams(
            collective_id=2, has_side_effects=True, dimension_semantics=("arbitrary",),
            vmem_limit_bytes=48 << 20),
        name="last_update",
    )(coefs, m, v, p, lhs0, lhs1, rhs0, rhs1, w, mom)


def backward(slopes, hidden, hidden_slope, up_pre, activated, slope):
    gate_slope = (hidden_slope * up_pre * slope).astype(jnp.bfloat16)
    up_slope = (hidden_slope * activated).astype(jnp.bfloat16)
    return jnp.stack([gate_slope.T, up_slope.T, hidden.T])


def body(n_isl, n_fsdp, weights, momentum, first_moment, second_moment, inputs, targets,
         overflow_step):
    moment_one = first_moment[0]
    moment_two = second_moment[0]
    rows = inputs.shape[1]
    width = inputs.shape[2]
    local_hidden = weights.shape[1]
    hidden_units = local_hidden * n_fsdp
    tokens = rows * n_fsdp
    scale_in, scale_out = 1.0 / math.sqrt(width), 1.0 / math.sqrt(hidden_units)

    down_weights = lax.all_gather(weights[2].astype(jnp.bfloat16), "isl", axis=1, tiled=True)
    line = lax.broadcasted_iota(jnp.int32, (8, 128), 0)
    flags = (line == overflow_step[0, 0]).astype(jnp.float32)
    every, counts = gather_inputs(inputs, flags, n_fsdp, n_isl)
    every = every.reshape(2, tokens, width)

    active = (counts[:, :2, 0] < 0.5).astype(jnp.float32)
    act0, act1 = active[0, 0], active[0, 1]
    shrink = inner_rate * decay_rate
    weight_part = jnp.sum(
        shrink * (active[:, 0] + active[:, 1]) - shrink * shrink * active[:, 0] * active[:, 1]
    ) / n_isl
    keep0, keep1 = 1.0 - shrink * act0, 1.0 - shrink * act1
    scales = jnp.array([scale_in, scale_in, scale_out], jnp.float32)
    zeros = jnp.zeros((3,), jnp.float32)
    root_second = math.sqrt(beta_second)
    coefs0 = jnp.stack([
        (1 - beta_first) / beta_first * scales,
        (1 - beta_second) / beta_second * scales * scales,
        zeros + epsilon / root_second,
        zeros + inner_rate * beta_first / root_second * act0,
    ], axis=1)
    one = 1.0 + (beta_first - 1.0) * act0
    two = 1.0 + (beta_second - 1.0) * act0
    root_two = jnp.sqrt(beta_second * two)
    coefs1 = jnp.stack([
        act0 * (1 - beta_first) / one * scales,
        (1 - beta_first) / (beta_first * one) * scales,
        act0 * (1 - beta_second) / two * scales * scales,
        (1 - beta_second) / (beta_second * two) * scales * scales,
        zeros + epsilon / root_two,
        zeros + inner_rate * act1 * beta_first * one / root_two,
        zeros + keep1,
        zeros + weight_part,
    ], axis=1)

    both = every.reshape(2 * tokens, width)
    by_owner = both.reshape(2 * tokens, n_isl, width // n_isl).transpose(1, 0, 2)
    gate_all, up_all = preactivations(by_owner, weights)

    def down(part):
        return part.astype(jnp.bfloat16).reshape(n_fsdp, rows, width)

    gate_pre, up_pre = gate_all[:tokens] * scale_in, up_all[:tokens] * scale_in
    activated, slope = silu_parts(gate_pre)
    hidden0 = (activated * up_pre).astype(jnp.bfloat16)
    part = jnp.dot(hidden0, down_weights, preferred_element_type=jnp.float32)
    slopes0 = island_slopes(down(part), inputs[0], targets[0], hidden_units)
    slopes0 = slopes0.reshape(tokens, width)
    hidden_slope = contract_last(slopes0, down_weights) * scale_out
    lhs0 = backward(slopes0, hidden0, hidden_slope, up_pre, activated, slope)
    rhs0 = jnp.stack([every[0], slopes0])
    step0, moved = first_update(coefs0, moment_one, moment_two, lhs0, rhs0, every[1])

    gate_pre = (keep0 * gate_all[tokens:] - moved[0].T) * scale_in
    up_pre = (keep0 * up_all[tokens:] - moved[1].T) * scale_in
    activated, slope = silu_parts(gate_pre)
    hidden1 = (activated * up_pre).astype(jnp.bfloat16)
    part = (keep0 * jnp.dot(hidden1, down_weights, preferred_element_type=jnp.float32)
            - jnp.dot(hidden1, step0[2], preferred_element_type=jnp.float32))
    slopes1 = island_slopes(down(part), inputs[1], targets[1], hidden_units)
    slopes1 = slopes1.reshape(tokens, width)
    hidden_slope = (keep0 * contract_last(slopes1, down_weights)
                    - contract_last(slopes1, step0[2])) * scale_out
    lhs1 = backward(slopes1, hidden1, hidden_slope, up_pre, activated, slope)
    rhs1 = jnp.stack([every[1], slopes1])
    return last_update(coefs1, moment_one, moment_two, step0, lhs0, lhs1, rhs0, rhs1,
                       weights, momentum)


def solution(mesh):
    in_specs = (
        P(None, "fsdp", "isl"),
        P(None, "fsdp", "isl"),
        P("isl", None, "fsdp", None),
        P("isl", None, "fsdp", None),
        P(None, ("isl", "fsdp"), None),
        P(None, ("isl", "fsdp"), None),
        P("isl", "fsdp"),
    )
    out_specs = (P(None, "fsdp", "isl"), P(None, "fsdp", "isl"))
    fn = functools.partial(body, mesh.shape["isl"], mesh.shape["fsdp"])
    return jax.shard_map(fn, mesh=mesh, in_specs=in_specs, out_specs=out_specs, check_vma=False)
```
